32 devices in a mesh: dp: 4 (over y, x), section: 2 (over core), tensor: 4 (over z).
Axes of the slice: x: 2, y: 2, z: 4, core: 2. Of those that a mesh axis runs over, the one named last changes fastest.
Arguments:
- stored: bfloat16 [2, 2, 256, 8192], P('section', None, 'dp', 'tensor'), may hold values from -6 to 6
- cotangent: bfloat16 [2, 32, 8192], P(None, None, 'tensor'), may hold values from -12 to 12
- positions: int32 [2, 32], replicated, may hold values from 128 to 255, as said below
- lengths: int32 [2], replicated, may hold values from 128 to 256, as said below
- norm_gain: float32 [2, 8192], P('section'), may hold values from 0.5 to 1.5
- w_query: bfloat16 [2, 8192, 8192], P('section', None, 'tensor')
- w_key: bfloat16 [2, 8192, 1024], P('section', None, 'tensor')
- w_value: bfloat16 [2, 8192, 1024], P('section', None, 'tensor'), may hold values from -0.0625 to 0.0625
- w_out: bfloat16 [2, 8192, 8192], P('section', 'tensor', 'dp'), may hold values from -0.0625 to 0.0625
Outputs:
- input_grads: float32 [2, 2, 256, 8192], P('section', None, 'dp', 'tensor')
The draws below stay inside these ranges and needn't reach their ends.
Inputs may be any that keep to these rules, and one draw needn't show every extreme that they name: In each sequence the response positions are distinct, rise along the last dimension, lie in the last 128 positions, and the last one is 255. `lengths`: some sequence has length 256.
All inputs are finite; a program needn't handle non-finite values.
Results may differ from the reference program's by a relative error of at most 0.017.
Values may be sent and summed in bfloat16 or wider, within the bound.
A program may use at most 256 MiB of HBM per device.

```python
import math
import jax
import jax.numpy as jnp
from jax import lax

D = 8192
HEADS = 64
KV = 8
HD = 128
RESP = 32
SEQS = 2
SEQ = 256
N_TENSOR = 4


def key_base(key):
    return jax.random.normal(jax.random.fold_in(key, 101), (2, D, KV * HD), jnp.float32) / math.sqrt(D)


def draw_w_key(key, part):
    base = key_base(key)
    return base.astype(jnp.bfloat16)


def draw_w_query(key, part):
    noise = jax.random.normal(jax.random.fold_in(key, 202), (2, D, HEADS * HD), jnp.float32) / math.sqrt(D)
    return noise.astype(jnp.bfloat16)


def length_draw(key):
    drawn = jax.random.randint(jax.random.fold_in(key, 404), (SEQS,), SEQ // 2, SEQ + 1)
    longest = jax.random.randint(jax.random.fold_in(key, 405), (), 0, SEQS)
    return jnp.where(jnp.arange(SEQS) == longest, SEQ, drawn).astype(jnp.int32)


def draw_lengths(key, part):
    return length_draw(key)


def draw_positions(key, part):
    span = 4 * RESP
    seq_keys = jax.random.split(jax.random.fold_in(key, 406), SEQS)
    picks = jax.vmap(lambda one_key: jnp.sort(jax.random.permutation(one_key, span - 1)[:RESP - 1]))(seq_keys)
    offsets = jnp.concatenate([picks, jnp.full((SEQS, 1), span - 1, jnp.int32)], 1)
    return (SEQ - span + offsets).astype(jnp.int32)


def block_levels(stream_key, shape, pieces, low, high):
    def one(axis_at, parts):
        heights = jax.random.uniform(jax.random.fold_in(jax.random.fold_in(stream_key, 6), axis_at), (parts,), jnp.float32, low / len(pieces), high / len(pieces))
        return jnp.repeat(jnp.exp(heights), shape[axis_at] // parts).reshape((-1,) + (1,) * (len(shape) - axis_at - 1))

    level = one(*pieces[0])
    for cut in pieces[1:]:
        level = level * one(*cut)
    return level


def scatter_about(key, dims, width, most, cuts=(), kind=jnp.bfloat16):
    entries = width * jax.random.normal(key, dims, jnp.float32)
    if cuts:
        entries = entries * block_levels(key, dims, cuts, -0.22, 0.18)
    return jnp.clip(entries, -most, most).astype(kind)


def setup_inputs(seed: int = 0) -> dict:
    seeds = jax.random.split(jax.random.key(seed), 10)
    return {
        "stored": scatter_about(seeds[0], (2, SEQS, SEQ, D), 1.0, 6.0, ((0, 2), (2, 4), (3, 4))),
        "cotangent": scatter_about(seeds[1], (SEQS, RESP, D), 2.0, 12.0, ((2, 4),)),
        "positions": draw_positions(jax.random.fold_in(seeds[9], 71), 0),
        "lengths": draw_lengths(jax.random.fold_in(seeds[9], 71), 0),
        "norm_gain": jnp.clip(1.0 + 0.1 * jax.random.normal(seeds[4], (2, D), jnp.float32), 0.5, 1.5),
        "w_query": draw_w_query(jax.random.fold_in(seeds[9], 71), 0),
        "w_key": draw_w_key(jax.random.fold_in(seeds[9], 71), 0),
        "w_value": scatter_about(seeds[7], (2, D, KV * HD), D ** -0.5, 0.0625, ((0, 2), (2, 4))),
        "w_out": scatter_about(seeds[8], (2, HEADS * HD, D), (HEADS * HD) ** -0.5, 0.0625, ((0, 2), (1, 4), (2, 4))),
    }


EPS = 1e-05
THETA = 500000.0

def angle_tables(count):
    half_dim = HD // 2
    frequency = THETA ** (-(jnp.arange(half_dim, dtype=jnp.float32) * 2.0) / HD)
    angles = jnp.arange(count, dtype=jnp.float32)[:, None] * frequency[None, :]
    cosine = jnp.concatenate([jnp.cos(angles), jnp.cos(angles)], -1)[:, None, :]
    sine_table = jnp.concatenate([jnp.sin(angles), jnp.sin(angles)], -1)[:, None, :]
    return (cosine, sine_table)

def turn_half(values):
    half_dim = values.shape[-1] // 2
    return jnp.concatenate([-values[..., half_dim:], values[..., :half_dim]], -1)

def rotate(values, cosine, sine_table):
    return values * cosine + turn_half(values) * sine_table

def unrotate(values, cosine, sine_table):
    return values * cosine - turn_half(values * sine_table)

def layer_grad(inputs, upstream, lengths, gain, w_query, w_key, w_value, w_out):
    q_cols = HEADS * HD // N_TENSOR
    kv_cols = KV * HD // N_TENSOR
    kv_dev = KV // N_TENSOR
    group = HEADS // KV
    scale = 1.0 / HD ** 0.5
    cosine, sine_table = angle_tables(SEQ)
    seq_ids = jnp.arange(SEQ, dtype=jnp.int32)

    def one_seq(packed):
        inputs_s, upstream_s, length_s = packed
        x_full = inputs_s.astype(jnp.float32)
        inv_rms = lax.rsqrt(lax.optimization_barrier(jnp.mean(x_full * x_full, -1, keepdims=True)) + EPS)
        normed = (x_full * inv_rms * gain).astype(jnp.bfloat16)
        start_pos = SEQ - length_s
        causal = seq_ids[None, :] <= seq_ids[:, None]
        valid = (seq_ids[None, :] >= start_pos) | (seq_ids[None, :] == seq_ids[:, None])
        allowed = causal & valid
        summed = jnp.zeros((SEQ, D), jnp.float32)
        for part in range(N_TENSOR):
            wq_part = w_query[:, part * q_cols:(part + 1) * q_cols]
            wk_part = w_key[:, part * kv_cols:(part + 1) * kv_cols]
            wv_part = w_value[:, part * kv_cols:(part + 1) * kv_cols]
            wo_part = w_out[part * q_cols:(part + 1) * q_cols, :]
            queries = jnp.dot(normed, wq_part, preferred_element_type=jnp.float32).reshape(SEQ, q_cols // HD, HD)
            keys = jnp.dot(normed, wk_part, preferred_element_type=jnp.float32).reshape(SEQ, kv_dev, HD)
            values = jnp.dot(normed, wv_part, preferred_element_type=jnp.float32).reshape(SEQ, kv_dev, HD)
            q_rot = rotate(queries, cosine, sine_table).astype(jnp.bfloat16)
            k_rot = rotate(keys, cosine, sine_table).astype(jnp.bfloat16).astype(jnp.float32)
            values_b = values.astype(jnp.bfloat16).astype(jnp.float32)
            grad_out = jnp.dot(upstream_s, wo_part.T, preferred_element_type=jnp.float32).astype(jnp.bfloat16)
            q_five = q_rot.reshape(SEQ, kv_dev, group, HD).astype(jnp.float32)
            o_five = grad_out.reshape(SEQ, kv_dev, group, HD).astype(jnp.float32)
            scores = jnp.einsum('pkgd,jkd->kgpj', q_five, k_rot) * scale
            masked = jnp.where(allowed, scores, -1e+30)
            highest = lax.optimization_barrier(jnp.max(masked, -1, keepdims=True))
            expo_terms = jnp.where(allowed, jnp.exp(masked - highest), 0.0)
            probs = expo_terms / lax.optimization_barrier(jnp.sum(expo_terms, -1, keepdims=True))
            grad_probs = jnp.einsum('pkgd,jkd->kgpj', o_five, values_b)
            row_dot = lax.optimization_barrier(jnp.sum(probs * grad_probs, -1, keepdims=True))
            grad_scores = (probs * (grad_probs - row_dot) * scale).astype(jnp.bfloat16).astype(jnp.float32)
            probs_b = probs.astype(jnp.bfloat16).astype(jnp.float32)
            grad_qr = jnp.einsum('kgpj,jkd->pkgd', grad_scores, k_rot).reshape(SEQ, q_cols // HD, HD)
            grad_kr = jnp.einsum('kgpj,pkgd->jkd', grad_scores, q_five)
            grad_vr = jnp.einsum('kgpj,pkgd->jkd', probs_b, o_five)
            grad_q = unrotate(grad_qr, cosine, sine_table).astype(jnp.bfloat16).reshape(SEQ, q_cols)
            grad_k = unrotate(grad_kr, cosine, sine_table).astype(jnp.bfloat16).reshape(SEQ, kv_cols)
            grad_v = grad_vr.astype(jnp.bfloat16).reshape(SEQ, kv_cols)
            partial_term = jnp.dot(grad_q, wq_part.T, preferred_element_type=jnp.float32)
            partial_term = partial_term + jnp.dot(grad_k, wk_part.T, preferred_element_type=jnp.float32)
            partial_term = partial_term + jnp.dot(grad_v, wv_part.T, preferred_element_type=jnp.float32)
            summed = summed + lax.optimization_barrier(partial_term.astype(jnp.bfloat16)).astype(jnp.float32)
        stat = lax.optimization_barrier(jnp.sum(x_full * gain * summed, -1, keepdims=True))
        return upstream_s.astype(jnp.float32) + inv_rms * gain * summed - x_full * inv_rms ** 3 * stat / D
    return lax.map(one_seq, (inputs, upstream, lengths))

def reference(stored, cotangent, positions, lengths, norm_gain, w_query, w_key, w_value, w_out):
    seq_ids = jnp.arange(SEQ, dtype=jnp.int32)
    hits = (positions[:, :, None] == seq_ids[None, None, :]).astype(jnp.float32)
    from_loss = jnp.einsum('srp,srd->spd', hits, cotangent.astype(jnp.float32)).astype(jnp.bfloat16)
    upper = layer_grad(stored[1], from_loss, lengths, norm_gain[1], w_query[1], w_key[1], w_value[1], w_out[1])
    lower = layer_grad(stored[0], upper.astype(jnp.bfloat16), lengths, norm_gain[0], w_query[0], w_key[0], w_value[0], w_out[0])
    return jnp.stack([lower, upper])
```

```python
import functools
import math

import jax
import jax.numpy as jnp
from jax import lax
from jax.experimental import pallas as pl
from jax.experimental.pallas import tpu as pltpu
from jax.sharding import PartitionSpec as P

HD = 128
EPS = 1e-05
THETA = 500000.0
BF = jnp.bfloat16
F32 = jnp.float32


def angle_tables(row_places):
    frequency = THETA ** (-(jnp.arange(HD // 2, dtype=F32) * 2.0) / HD)
    angles = row_places[..., None] * frequency
    cosine = jnp.concatenate([jnp.cos(angles)] * 2, -1)
    sine = jnp.concatenate([jnp.sin(angles)] * 2, -1)
    return cosine, sine


def turn_half(values):
    half = values.shape[-1] // 2
    return jnp.concatenate([-values[..., half:], values[..., :half]], -1)


def rotate(values, cosine, sine):
    return values * cosine + turn_half(values) * sine


def unrotate(values, cosine, sine):
    return values * cosine - turn_half(values * sine)


def shift(value, axis, step, source=None, target=None):
    count = lax.axis_size(axis)
    if source is None:
        return lax.ppermute(value, axis, [(a, (a + step) % count) for a in range(count)])
    if axis == "dp":
        sections = lax.axis_size("section")
        pairs = [(a * sections + source, (a + step) % count * sections + target) for a in range(count)]
        return lax.ppermute(value, ("dp", "section"), pairs)
    pairs = [(source * count + a, target * count + (a + step) % count) for a in range(count)]
    return lax.ppermute(value, ("section", axis), pairs)


def scatter_sum(piece, axis, section=None):
    count = lax.axis_size(axis)
    me = lax.axis_index(axis)
    order = sorted(range(1, count), key=lambda s: -min(s, count - s))
    arrived = [shift(piece((me + s) % count), axis, s, section, section) for s in order]
    total = piece(me).astype(F32)
    for term in arrived:
        total = total + term.astype(F32)
    return total


def gather(value, axis):
    count = lax.axis_size(axis)
    me = lax.axis_index(axis)
    got = [value] + [shift(value, axis, s) for s in range(1, count)]
    return got, me


def by_device(got, me):
    count = len(got)
    stacked = jnp.stack(got)
    return stacked[(me - jnp.arange(count)) % count]


def attention_kernel(group, q_ref, o_ref, k_ref, v_ref, info_ref, cos_ref, sin_ref, gq_ref, gk_ref, gv_ref):
    scale = 1.0 / math.sqrt(HD)
    rows = q_ref.shape[1]
    keys, values = k_ref[0], v_ref[0]
    length = keys.shape[0]

    def heads(ref):
        return jnp.concatenate([ref[0, :, h * HD : (h + 1) * HD] for h in range(group)], 0)

    q, o = heads(q_ref), heads(o_ref)
    info = jnp.concatenate([info_ref[0]] * group, 0)
    place, start = info[:, 0:1], info[:, 1:2]
    key_ids = lax.broadcasted_iota(jnp.int32, (rows * group, length), 1)
    allowed = (key_ids == place) | ((key_ids < place) & (key_ids >= start))
    contract = (((1,), (1,)), ((), ()))
    scores = lax.dot_general(q, keys, contract, preferred_element_type=F32) * scale
    masked = jnp.where(allowed, scores, -1e30)
    highest = jnp.max(masked, -1, keepdims=True)
    expo = jnp.where(allowed, jnp.exp(masked - highest), 0.0)
    probs = expo / jnp.sum(expo, -1, keepdims=True)
    grad_probs = lax.dot_general(o, values, contract, preferred_element_type=F32)
    row_dot = jnp.sum(probs * grad_probs, -1, keepdims=True)
    grad_scores = (probs * (grad_probs - row_dot) * scale).astype(BF)
    over_rows = (((0,), (0,)), ((), ()))
    gk_ref[0] = lax.dot_general(grad_scores, q, over_rows, preferred_element_type=F32)
    gv_ref[0] = lax.dot_general(probs.astype(BF), o, over_rows, preferred_element_type=F32)
    gq = jnp.dot(grad_scores, keys, preferred_element_type=F32)
    cosine, sine = cos_ref[0], sin_ref[0]
    lane = lax.broadcasted_iota(jnp.int32, (rows, HD), 1)
    sign = jnp.where(lane < HD // 2, -1.0, 1.0).astype(F32)
    for h in range(group):
        one = gq[h * rows : (h + 1) * rows]
        turned = pltpu.roll(one * sine, HD // 2, 1) * sign
        gq_ref[0, :, h * HD : (h + 1) * HD] = (one * cosine - turned).astype(BF)


def attention_grad(q, o, k, v, places, starts, cosine, sine):
    batch, rows, q_cols = q.shape
    length, kv_cols = k.shape[1:]
    kv = kv_cols // HD
    group = q_cols // kv_cols
    info = jnp.stack([places, jnp.broadcast_to(starts[:, None], places.shape)], -1)
    wide = pl.BlockSpec((1, rows, group * HD), lambda b, h: (b, 0, h))
    tall = pl.BlockSpec((1, length, HD), lambda b, h: (b, 0, h))
    table = pl.BlockSpec((1, rows, HD), lambda b, h: (b, 0, 0))
    pairs = batch * kv * group * rows * length
    return pl.pallas_call(
        functools.partial(attention_kernel, group),
        grid=(batch, kv),
        in_specs=[wide, wide, tall, tall, pl.BlockSpec((1, rows, 2), lambda b, h: (b, 0, 0)), table, table],
        out_specs=[wide, tall, tall],
        out_shape=[
            jax.ShapeDtypeStruct((batch, rows, q_cols), BF),
            jax.ShapeDtypeStruct((batch, length, kv_cols), F32),
            jax.ShapeDtypeStruct((batch, length, kv_cols), F32),
        ],
        cost_estimate=pl.CostEstimate(flops=10 * pairs * HD, bytes_accessed=8 * q.size, transcendentals=pairs),
    )(q, o, k, v, info, cosine, sine)


def matmul_t(a, w):
    return lax.dot_general(a, w, (((a.ndim - 1,), (1,)), ((), ())), preferred_element_type=F32)


def on_device(stored, cotangent, positions, lengths, norm_gain, w_query, w_key, w_value, w_out):
    own_x = stored[0]
    gain, wq, wk, wv, wo = norm_gain[0], w_query[0], w_key[0], w_value[0], w_out[0]
    seqs, rows, width_dev = own_x.shape
    resp = positions.shape[1]
    q_cols, kv_cols = wq.shape[1], wk.shape[1]
    kv_dev, q_dev = kv_cols // HD, q_cols // HD
    n_dp, n_tensor = lax.axis_size("dp"), lax.axis_size("tensor")
    dp, tensor, section = lax.axis_index("dp"), lax.axis_index("tensor"), lax.axis_index("section")
    length = rows * n_dp
    width = width_dev * n_tensor
    starts = length - lengths
    flat = seqs * rows
    row_ids = dp * rows + jnp.arange(rows, dtype=jnp.int32)
    placed = (positions[:, None, :] == row_ids[None, :, None]).astype(BF)

    cot_width = wo.shape[1]
    if n_dp == n_tensor:
        pairs = [(d * n_tensor + t, t * n_tensor + d) for d in range(n_dp) for t in range(n_tensor)]
        cot = lax.ppermute(cotangent, ("dp", "tensor"), pairs)
    else:
        cot = lax.all_gather(cotangent, "tensor", axis=2, tiled=True)
        cot = lax.dynamic_slice_in_dim(cot, dp * cot_width, cot_width, 2)
    term = matmul_t(cot.reshape(seqs * resp, cot_width), wo).astype(BF)
    got, _ = gather(term, "dp")
    upper_out = functools.reduce(lambda a, b: a + b, [g.astype(F32) for g in got]).astype(BF)
    upper_out = upper_out.reshape(seqs, resp, q_cols)

    x_full = lax.all_gather(own_x, "tensor", axis=2, tiled=True).astype(F32)
    inv_rms = lax.rsqrt(jnp.mean(x_full * x_full, -1, keepdims=True) + EPS)
    normed = (x_full * inv_rms * gain).astype(BF).reshape(flat, width)
    queries = jnp.dot(normed, wq, preferred_element_type=F32)
    keys = jnp.dot(normed, wk, preferred_element_type=F32)
    values = jnp.dot(normed, wv, preferred_element_type=F32)
    cosine, sine = angle_tables(row_ids.astype(F32))
    c4, s4 = cosine[None, :, None, :], sine[None, :, None, :]
    q_rot = rotate(queries.reshape(seqs, rows, q_dev, HD), c4, s4).astype(BF).reshape(seqs, rows, q_cols)
    k_rot = rotate(keys.reshape(seqs, rows, kv_dev, HD), c4, s4).astype(BF).reshape(seqs, rows, kv_cols)
    kv = jnp.concatenate([k_rot, values.astype(BF).reshape(seqs, rows, kv_cols)], -1)
    q_picked = jnp.einsum("bpr,bpc->brc", placed, q_rot, preferred_element_type=F32).astype(BF)

    got, me = gather(q_picked, "dp")
    upper_q = functools.reduce(lambda a, b: a + b, got)
    got, me = gather(kv, "dp")
    all_kv = by_device(got, me).transpose(1, 0, 2, 3).reshape(seqs, length, 2 * kv_cols)
    all_k, all_v = all_kv[..., :kv_cols], all_kv[..., kv_cols:]

    def input_grad(grad_q, grad_k, grad_v, upstream, sect):
        lhs_q = grad_q.reshape(flat, q_cols)
        lhs_k = grad_k.reshape(flat, kv_cols)
        lhs_v = grad_v.reshape(flat, kv_cols)

        def piece(j):
            def part(w):
                return lax.dynamic_slice_in_dim(w, j * width_dev, width_dev, 0)

            out = matmul_t(lhs_q, part(wq)) + matmul_t(lhs_k, part(wk)) + matmul_t(lhs_v, part(wv))
            return out.astype(BF)

        stat = (
            jnp.sum(lhs_q.astype(F32) * queries, -1)
            + jnp.sum(lhs_k.astype(F32) * keys, -1)
            + jnp.sum(lhs_v.astype(F32) * values, -1)
        ).reshape(seqs, rows)
        got, _ = gather(stat, "tensor")
        stat = functools.reduce(lambda a, b: a + b, got)[..., None]
        summed = scatter_sum(piece, "tensor", sect).reshape(seqs, rows, width_dev)
        own_gain = lax.dynamic_slice_in_dim(gain, tensor * width_dev, width_dev, 0)
        return upstream.astype(F32) + inv_rms * own_gain * summed - own_x.astype(F32) * inv_rms**2 * stat / width

    cos_r, sin_r = angle_tables(positions.astype(F32))
    gq, gk, gv = attention_grad(upper_q, upper_out, all_k, all_v, positions, starts, cos_r, sin_r)
    gq = jnp.einsum("bpr,brc->bpc", placed, gq, preferred_element_type=F32).astype(BF)

    def own_kv_grads(gk, gv):
        gk = unrotate(gk.reshape(seqs, rows, kv_dev, HD), c4, s4).astype(BF)
        return gk.reshape(seqs, rows, kv_cols), gv.astype(BF)

    gk = lax.dynamic_slice_in_dim(gk, dp * rows, rows, 1)
    gv = lax.dynamic_slice_in_dim(gv, dp * rows, rows, 1)
    from_loss = jnp.einsum("bpr,brd->bpd", placed, cotangent, preferred_element_type=F32).astype(BF)
    upper = input_grad(gq, *own_kv_grads(gk, gv), from_loss, 1)

    handed_block = upper.astype(BF)
    blocks = [shift(handed_block, "tensor", s, 1, 0) for s in range(n_tensor)]
    handed = blocks[0]
    stacked = jnp.stack(blocks)
    if n_dp == n_tensor:

        def columns(j):
            return stacked[(tensor - j) % n_tensor]
    else:
        whole = by_device(blocks, tensor).transpose(1, 2, 0, 3).reshape(seqs, rows, width)

        def columns(j):
            return lax.dynamic_slice_in_dim(whole, j * cot_width, cot_width, 2)

    out_sum = 0.0
    for s in range(n_dp):
        block = columns((dp + s) % n_dp)
        if s:
            block = shift(block, "dp", s, 0, 0)
        term = matmul_t(block.reshape(flat, cot_width), wo)
        if s:
            term = shift(term.astype(BF), "dp", -s, 0, 0).astype(F32)
        out_sum = out_sum + term
    lower_out = out_sum.astype(BF).reshape(seqs, rows, q_cols)
    places = jnp.broadcast_to(row_ids[None, :], (seqs, rows))
    wide = (seqs, rows, HD)
    gq, gk, gv = attention_grad(
        q_rot, lower_out, all_k, all_v, places, starts, jnp.broadcast_to(cosine, wide), jnp.broadcast_to(sine, wide)
    )
    packed = jnp.concatenate([gk, gv], -1).astype(BF)
    own = scatter_sum(lambda j: lax.dynamic_slice_in_dim(packed, j * rows, rows, 1), "dp", 0)
    lower = input_grad(gq, *own_kv_grads(own[..., :kv_cols], own[..., kv_cols:]), handed, 0)
    return jnp.where(section == 0, lower, upper)[None]


def solution(mesh):
    return jax.shard_map(
        on_device,
        mesh=mesh,
        in_specs=(
            P("section", None, "dp", "tensor"),
            P(None, None, "tensor"),
            P(),
            P(),
            P("section", None),
            P("section", None, "tensor"),
            P("section", None, "tensor"),
            P("section", None, "tensor"),
            P("section", "tensor", "dp"),
        ),
        out_specs=P("section", None, "dp", "tensor"),
        check_vma=False,
    )
```
